768 devices in a mesh: dp: 96 (over z_lo, y, core), expert: 8 (over x, z_hi).
Axes of the slice: x: 4, y: 8, z: 12 (z_hi: 2, z_lo: 6; z = z_hi * 6 + z_lo), core: 2. Of those that a mesh axis runs over, the one named last changes fastest.
Arguments:
- grad_out: bfloat16 [196608, 3072], P(('dp', 'expert')), may hold values from -1.5 to 1.5
- routes: int32 [196608, 2], P(('dp', 'expert')), may hold values from 0 to 63, as said below
- gate_levels: int32 [196608, 2], P(('dp', 'expert')), may hold values from 1 to 15
- saved_inputs: bfloat16 [73728, 3072], P(('dp', 'expert')), may hold values from -6 to 6
- w_gate: bfloat16 [3072, 2048], P(None, 'expert'), may hold values from -0.109375 to 0.109375
- w_up: bfloat16 [3072, 2048], P(None, 'expert'), may hold values from -0.109375 to 0.109375
- w_down: bfloat16 [2048, 3072], P('expert'), may hold values from -0.1875 to 0.1875
Outputs:
- input_grad: bfloat16 [196608, 3072], P(('dp', 'expert'))
- gate_grad: float32 [196608, 2], P(('dp', 'expert'))
- weight_grad: float32 [3072, 3, 2048], P('dp', None, 'expert')
The draws below stay inside these ranges and needn't reach their ends.
Inputs may be any that keep to these rules, and one draw needn't show every extreme that they name: `routes`: the ids of one token differ. A device's tokens name each expert below 2 at most 12 times; in every block one of them is named exactly 12 times, and the same one for all 8 blocks of one replica.
All inputs are finite; a program needn't handle non-finite values.
Results may differ from the reference program's by a relative error of at most 0.012.
Values may be sent and summed in bfloat16 or wider, within the bound.
A program may use at most 128 MiB of HBM per device.

```python
import jax
import jax.numpy as jnp
from jax import lax

D = 3072
FF = 1024
EXPERTS_ALL = 64
EXPERTS_W = 2
CAP = 12
TOK_DEV = 256
GROUP = 8
F_DEV = 256
TOKENS = 196608
SLOTS = 73728
N_DP = 96
N_EXPERT = 8


def draw_routes(key, part):
    blocks = TOKENS // TOK_DEV
    keys = jax.random.split(key, 6)
    shift = jax.random.randint(keys[0], (), 0, 2)
    block_ids = jnp.arange(blocks, dtype=jnp.int32)
    full_one = (block_ids // GROUP + shift) % 2
    other_count = jax.random.randint(keys[1], (blocks,), 1, CAP + 1)
    count_zero = jnp.where(full_one == 0, CAP, other_count)
    count_one = jnp.where(full_one == 1, CAP, other_count)
    scores = jax.random.randint(keys[2], (blocks, TOK_DEV), 0, 1 << 20) * TOK_DEV + jnp.arange(TOK_DEV, dtype=jnp.int32)
    position = jnp.argsort(jnp.argsort(scores, axis=1), axis=1)
    outside = 2 + jax.random.randint(keys[3], (blocks, TOK_DEV), 0, EXPERTS_ALL - 2)
    first = jnp.where(position < count_zero[:, None], 0, jnp.where(position < (count_zero + count_one)[:, None], 1, outside))
    offset = jax.random.randint(keys[4], (blocks, TOK_DEV), 0, EXPERTS_ALL - 3)
    second = jnp.where(first >= 2, 2 + (first - 2 + 1 + offset) % (EXPERTS_ALL - 2), 2 + offset)
    swapped = jax.random.randint(keys[5], (blocks, TOK_DEV), 0, 2)
    left = jnp.where(swapped == 1, second, first)
    right = jnp.where(swapped == 1, first, second)
    return jnp.stack([left, right], axis=2).reshape(TOKENS, 2).astype(jnp.int32)


def set_ends(result, own_key, least, top_value):
    index_at = [jax.random.randint(jax.random.fold_in(own_key, axis), (), 0, length) for axis, length in enumerate(result.shape)]
    longest = result.shape.index(max(result.shape))
    neighbour = index_at[:longest] + [(index_at[longest] + 1) % result.shape[longest]] + index_at[longest + 1:]
    return result.at[tuple(index_at)].set(least).at[tuple(neighbour)].set(top_value)


def block_scale(rng, shape, cuts, low, top_value):
    loudness, own = 1.0, jax.random.fold_in(rng, 6)
    for dim, shards_of in cuts:
        steps = jnp.exp(jax.random.uniform(jax.random.fold_in(own, dim), (shards_of,), jnp.float32, low / len(cuts), top_value / len(cuts)))
        loudness = loudness * jnp.repeat(steps, shape[dim] // shards_of).reshape([-1 if axis == dim else 1 for axis in range(len(shape))])
    return loudness


def bell_draw(own_key, shape, deviation, reach, cuts=(), held_as=jnp.bfloat16):
    drawn = jax.random.normal(own_key, shape, jnp.float32) * deviation
    if len(cuts) > 0:
        drawn = block_scale(own_key, shape, cuts, -0.22, 0.18) * drawn
    return jnp.clip(drawn, min=-reach, max=reach).astype(held_as)


def setup_inputs(seed: int = 0) -> dict:
    streams_of = jax.random.split(jax.random.key(seed), 8)
    return {
        "grad_out": bell_draw(streams_of[0], (TOKENS, D), 0.25, 1.5, ((0, 768),)),
        "routes": draw_routes(jax.random.fold_in(streams_of[7], 71), 0),
        "gate_levels": set_ends(jax.random.randint(streams_of[2], (TOKENS, 2), 1, 16), jax.random.fold_in(streams_of[2], 1), 1, 15).astype(jnp.int32),
        "saved_inputs": bell_draw(streams_of[3], (SLOTS, D), 1.0, 6.0, ((0, 768),)),
        "w_gate": bell_draw(streams_of[4], (D, N_EXPERT * F_DEV), D ** -0.5, 0.109375, ((1, 8),)),
        "w_up": bell_draw(streams_of[5], (D, N_EXPERT * F_DEV), D ** -0.5, 0.109375, ((1, 8),)),
        "w_down": bell_draw(streams_of[6], (N_EXPERT * F_DEV, D), FF ** -0.5, 0.1875, ((0, 8),)),
    }


def reference(grad_out, routes, gate_levels, saved_inputs, w_gate, w_up, w_down):
    group = N_EXPERT
    shards = group // EXPERTS_W
    f_dev = FF // shards
    blocks_out = grad_out.reshape(N_DP, group, TOK_DEV, D)
    route_blocks = routes.reshape(N_DP, group, TOK_DEV, 2)
    level_blocks = gate_levels.reshape(N_DP, group, TOK_DEV, 2)
    saved_blocks = saved_inputs.reshape(N_DP, group, group * CAP, D)
    gate_mats = w_gate.reshape(D, group, f_dev).transpose(1, 0, 2).astype(jnp.float32)
    up_mats = w_up.reshape(D, group, f_dev).transpose(1, 0, 2).astype(jnp.float32)
    down_mats = w_down.reshape(group, f_dev, D).astype(jnp.float32)
    owner = jnp.arange(group) // shards

    def one_row(carry, inputs):
        grads_row, routes_row, levels_row, saved_row = inputs
        hits = (routes_row[..., None] == jnp.arange(EXPERTS_W, dtype=jnp.int32)).astype(jnp.int32)
        member = jnp.sum(hits, axis=2)
        levels = jnp.sum(hits * levels_row[..., None], axis=2)
        slots = jnp.cumsum(member, axis=1) - 1
        placed = (member[..., None] == 1) & (slots[..., None] == jnp.arange(CAP, dtype=jnp.int32))
        token_index = jnp.sum(placed.astype(jnp.int32) * jnp.arange(TOK_DEV, dtype=jnp.int32)[None, :, None, None], axis=1)
        filled = jnp.any(placed, axis=1)
        flat_index = token_index.reshape(group, EXPERTS_W * CAP)
        picked = jnp.take_along_axis(grads_row, flat_index[:, :, None], axis=1).reshape(group, EXPERTS_W, CAP, D)
        picked = jnp.where(filled[..., None], picked, jnp.zeros_like(picked)).astype(jnp.bfloat16)
        level_slots = jnp.take_along_axis(jnp.transpose(levels, (0, 2, 1)), token_index, axis=2)
        slot_gate = jnp.where(filled, level_slots.astype(jnp.float32) / 16.0, jnp.float32(0.0))
        grad_rows = picked[:, owner].transpose(1, 0, 2, 3).reshape(group, group * CAP, D).astype(jnp.float32)
        gates = slot_gate[:, owner].transpose(1, 0, 2).reshape(group, group * CAP, 1)
        input_rows = saved_row.astype(jnp.float32)
        pre_gate = jnp.einsum("jrd,jdf->jrf", input_rows, gate_mats)
        pre_up = jnp.einsum("jrd,jdf->jrf", input_rows, up_mats)
        projected = jnp.einsum("jrd,jfd->jrf", grad_rows, down_mats)
        sigma = jax.nn.sigmoid(pre_gate)
        activ = pre_gate * sigma
        hidden = activ * pre_up
        gate_part = jnp.sum(hidden * projected, axis=2).astype(jnp.bfloat16)
        d_hidden = gates * projected
        d_up = (d_hidden * activ).astype(jnp.bfloat16)
        d_pre = (d_hidden * pre_up * sigma * (1.0 + pre_gate * (1.0 - sigma))).astype(jnp.bfloat16)
        scaled_hidden = (gates * hidden).astype(jnp.bfloat16)
        input_part = (jnp.einsum("jrf,jdf->jrd", d_pre.astype(jnp.float32), gate_mats)
                      + jnp.einsum("jrf,jdf->jrd", d_up.astype(jnp.float32), up_mats)).astype(jnp.bfloat16)
        term = jnp.stack([
            jnp.einsum("jrd,jrf->jdf", input_rows, d_pre.astype(jnp.float32)),
            jnp.einsum("jrd,jrf->jdf", input_rows, d_up.astype(jnp.float32)),
            jnp.einsum("jrd,jrf->jdf", grad_rows, scaled_hidden.astype(jnp.float32))], axis=2)
        carry = carry + term
        back = input_part.astype(jnp.float32).reshape(EXPERTS_W, shards, group, CAP, D).sum(axis=1).transpose(1, 0, 2, 3)
        gate_back = gate_part.astype(jnp.float32).reshape(EXPERTS_W, shards, group, CAP).sum(axis=1).transpose(1, 0, 2)
        clipped = jnp.transpose(jnp.clip(slots, 0, CAP - 1), (0, 2, 1))
        member_t = jnp.transpose(member, (0, 2, 1)).astype(jnp.float32)
        taken = jnp.take_along_axis(back, clipped[..., None], axis=2) * member_t[..., None]
        input_tok = jnp.sum(taken, axis=1).astype(jnp.bfloat16)
        per_expert = jnp.take_along_axis(gate_back, clipped, axis=2) * member_t
        gate_tok = jnp.sum(hits.astype(jnp.float32) * jnp.transpose(per_expert, (0, 2, 1))[:, :, None, :], axis=3)
        return carry, (input_tok, gate_tok)

    start = jnp.zeros((group, D, 3, f_dev), jnp.float32)
    total, (input_all, gate_all) = lax.scan(one_row, start, (blocks_out, route_blocks, level_blocks, saved_blocks))
    weight_grad = total.transpose(1, 2, 0, 3).reshape(D, 3, group * f_dev)
    return input_all.reshape(TOKENS, D), gate_all.reshape(TOKENS, 2), weight_grad
```

```python
import functools

import jax
import jax.numpy as jnp
from jax import lax
from jax.experimental import pallas as pl
from jax.experimental.pallas import tpu as pltpu
from jax.sharding import PartitionSpec as P

NY, NC, NH = 8, 2, 2
SLAB = 16
LANES = 128
BF, F32 = jnp.bfloat16, jnp.float32


def nt(a, b):
    return lax.dot_general(a, b, (((1,), (1,)), ((), ())), preferred_element_type=F32)


def nn(a, b):
    return lax.dot_general(a, b, (((1,), (0,)), ((), ())), preferred_element_type=F32)


def kernel(
    nx, nz, cap,
    routes_ref, levels_ref, go_hbm, x_hbm, wg_hbm, wu_hbm, wd_hbm,
    ig_hbm, gg_ref, wgr_ref,
    go, xv, wg, wu, wd, ig,
    pl_ref, plt_ref, pk, zin, dyin, xp, xt, xty, act, hid, dfac,
    nar, gp_in, gm_in, g4_in, dab, hg, ip, ret, zsum, zrin, dyt,
    gds, gdr, gdo, psend, prr, msend, mrr, p0r, m0r, sd, gx, gxr, sx,
    zsd, zrd, zsx, zrx, loc_sem, send_sem, recv_sem,
):
    dp, ex = lax.axis_index("dp"), lax.axis_index("expert")
    core = lax.rem(dp, NC)
    y = lax.rem(lax.div(dp, NC), NY)
    z = lax.div(dp, NC * NY)
    h = lax.rem(ex, NH)
    x = lax.div(ex, NH)
    width = go.shape[1]
    rows = dyin.shape[0] * SLAB
    zw = width // nz
    yw = zw // NY
    cw = yw // NC
    half = nz * cw // 2

    def x_dev(d):
        return (dp, lax.rem(x + d, nx) * NH + h)

    h_dev = (dp, x * NH + (1 - h))

    def y_dev(d):
        return ((z * NY + lax.rem(y + d, NY)) * NC + core, ex)

    c_dev = ((z * NY + y) * NC + (1 - core), ex)

    def z_dev(d):
        return ((lax.rem(z + d, nz) * NY + y) * NC + core, ex)

    started = []

    def send(src, dst, dev):
        i = len(started)
        copy = pltpu.make_async_remote_copy(
            src_ref=src, dst_ref=dst, send_sem=send_sem.at[i], recv_sem=recv_sem.at[i],
            device_id=dev, device_id_type=pl.DeviceIdType.MESH,
        )
        copy.start()
        started.append(copy)
        return copy

    loads = [
        pltpu.make_async_copy(src, dst, loc_sem.at[i])
        for i, (src, dst) in enumerate(
            [(go_hbm, go), (x_hbm, xv), (wg_hbm, wg), (wu_hbm, wu), (wd_hbm, wd)]
        )
    ]
    for load in loads:
        load.start()
    barrier = pltpu.get_barrier_semaphore()
    partners = (
        [h_dev] + [x_dev(d) for d in range(1, nx)] + [y_dev(d) for d in range(1, NY)]
        + [c_dev] + [z_dev(d) for d in range(1, nz)]
    )
    for dev in partners:
        pl.semaphore_signal(barrier, inc=1, device_id=dev, device_id_type=pl.DeviceIdType.MESH)

    toks = go.shape[0]
    r = routes_ref[...]
    lv = levels_ref[...].astype(F32)
    r0, r1, l0, l1 = r[0:1], r[1:2], lv[0:1], lv[1:2]
    mem = [jnp.where((r0 == e) | (r1 == e), 1.0, 0.0) for e in range(2)]
    lev = [jnp.where(r0 == e, l0, 0.0) + jnp.where(r1 == e, l1, 0.0) for e in range(2)]
    row8 = lax.broadcasted_iota(jnp.int32, (8, toks), 0)
    m8 = jnp.where(row8 == 0, mem[0], jnp.where(row8 == 1, mem[1], 0.0)).astype(BF)
    tri = jnp.where(
        lax.broadcasted_iota(jnp.int32, (toks, toks), 0)
        <= lax.broadcasted_iota(jnp.int32, (toks, toks), 1), 1.0, 0.0,
    ).astype(BF)
    slots = nn(m8, tri) - 1.0
    row = lax.broadcasted_iota(jnp.int32, (2 * SLAB, toks), 0)
    first = row < SLAB
    want = jnp.where(first, row, row - SLAB).astype(F32)
    slot_row = jnp.where(first, slots[0:1], slots[1:2])
    mem_row = jnp.where(first, mem[0], mem[1])
    lev_row = jnp.where(first, lev[0], lev[1])
    placed = jnp.where((mem_row > 0.5) & (slot_row == want), 1.0, 0.0)
    pl_ref[...] = placed
    gate = jnp.sum(placed * lev_row, axis=1, keepdims=True) * (1.0 / 16.0)
    pk[:, width:] = jnp.broadcast_to(gate, (2 * SLAB, LANES)).astype(BF)
    placed_b = placed.astype(BF)
    loads[0].wait()
    for c in range(0, width, 512):
        pk[:, c:c + 512] = nn(placed_b, go[:, c:c + 512]).astype(BF)

    cols = [(0, width // 2), (width // 2, width // 2 + LANES)]
    mine, other = x * NH + h, x * NH + (1 - h)
    pl.semaphore_wait(barrier, len(partners))
    z_in = [send(pk.at[:, pl.ds(a, w)], zin.at[:, pl.ds(a, w)], h_dev) for a, w in cols]

    def spread(src, slab, a, w):
        got = []
        for d in range(1, nx):
            e = lax.div(lax.rem(x + d, nx), nx // 2)
            lo = pl.multiple_of(e * SLAB, SLAB)
            got.append(send(src.at[pl.ds(lo, SLAB), pl.ds(a, w)],
                            dyin.at[slab, :, pl.ds(a, w)], x_dev(d)))
        return got

    own = pl.multiple_of(lax.div(x, nx // 2) * SLAB, SLAB)
    dy_own = [spread(pk, mine, a, w) for a, w in cols]
    dyin[mine] = pk[pl.ds(own, SLAB), :]

    loads[1].wait()
    n_rows = xv.shape[0]
    pad = jnp.zeros((LANES - n_rows, zw), BF)
    for b in range(nz):
        xt[b] = jnp.concatenate([xv[:, b * zw:(b + 1) * zw], pad], axis=0).T
    x_in = []
    for d in range(1, NY):
        lo = pl.multiple_of(lax.rem(y + d, NY) * yw, yw)
        x_in.append(send(xt.at[:, pl.ds(lo, yw), :], xty.at[d - 1], y_dev(d)))
    gi = lax.broadcasted_iota(jnp.int32, (rows, n_rows), 0)
    gk = lax.broadcasted_iota(jnp.int32, (rows, n_rows), 1)
    gc = jnp.bitwise_and(gi, SLAB - 1)
    gs = jnp.right_shift(gi, 4)
    widen = jnp.where((gc < cap) & (gk == gs * cap + gc), 1.0, 0.0).astype(BF)
    ni = lax.broadcasted_iota(jnp.int32, (n_rows, rows), 0)
    nk = lax.broadcasted_iota(jnp.int32, (n_rows, rows), 1)
    nc_ = jnp.bitwise_and(nk, SLAB - 1)
    ns = jnp.right_shift(nk, 4)
    narrow = jnp.where((nc_ < cap) & (ni == ns * cap + nc_), 1.0, 0.0).astype(BF)
    for c in range(0, width, 512):
        xp[:, c:c + 512] = nn(widen, xv[:, c:c + 512]).astype(BF)
    loads[2].wait()
    a_pre = nn(xp[...], wg[...])
    loads[3].wait()
    b_pre = nn(xp[...], wu[...])
    sigma = jax.nn.sigmoid(a_pre)
    activ = a_pre * sigma
    act[...] = activ
    hid[...] = activ * b_pre
    dfac[...] = b_pre * sigma * (1.0 + a_pre * (1.0 - sigma))
    pl_two = jnp.concatenate(
        [pl_ref[...], pl_ref[...], jnp.zeros((LANES - 4 * SLAB, toks), F32)], axis=0)
    plt_ref[...] = pl_two.T.astype(BF)

    dy_other = []
    for k, (a, w) in enumerate(cols):
        z_in[k].wait_recv()
        dy_other.append(spread(zin, other, a, w))
    dyin[other] = zin[pl.ds(own, SLAB), :]
    loads[4].wait()
    proj = jnp.zeros((rows, wd.shape[0]), F32)
    for k, (a, w) in enumerate(cols):
        for copy in dy_own[k] + dy_other[k]:
            copy.wait_recv()
        for c in range(a, a + width // 2, 512):
            proj += nt(dyin[:, :, c:c + 512].reshape(rows, 512), wd[:, c:c + 512])
    g_half = dyin[:, :, width:].reshape(rows, LANES).astype(F32)
    g = jnp.concatenate([g_half, g_half], axis=1)
    d_hid = g * proj
    dab[:, 256:] = (d_hid * act[...]).astype(BF)
    dab[:, :256] = (d_hid * dfac[...]).astype(BF)
    hg[...] = (g * hid[...]).astype(BF)
    gate_part = jnp.sum(hid[...] * proj, axis=1, keepdims=True).astype(BF)

    nar[...] = nn(narrow, dab[...]).astype(BF)
    hr = n_rows // 2
    up = [send(nar, gp_in.at[0], y_dev(1))]
    down = [send(nar, gm_in.at[0], y_dev(NY - 1))]

    for c in range(0, width, 512):
        part = nt(dab[:, :256], wg[c:c + 512, :]) + nt(dab[:, 256:], wu[c:c + 512, :])
        ip[:, :, c:c + 512] = part.astype(BF).reshape(dyin.shape[0], SLAB, 512)
    ip[:, :, width:] = jnp.broadcast_to(gate_part, (rows, LANES)).reshape(dyin.shape[0], SLAB, LANES)
    back = [[], []]
    for k, hh in enumerate((1 - h, h)):
        for d in range(1, nx):
            back[k].append(send(ip.at[lax.rem(x + d, nx) * NH + hh], ret.at[x, k], x_dev(d)))
        ret[x, k] = ip[x * NH + hh]

    def pass_on(k):
        up[k].wait_recv()
        down[k].wait_recv()
        if k < 2:
            up.append(send(gp_in.at[k], gp_in.at[k + 1], y_dev(1)))
            down.append(send(gm_in.at[k], gm_in.at[k + 1], y_dev(NY - 1)))
        else:
            up.append(send(gp_in.at[k, pl.ds(0, hr)], g4_in.at[pl.ds(0, hr)], y_dev(1)))
            down.append(send(gm_in.at[k, pl.ds(hr, hr)], g4_in.at[pl.ds(hr, hr)], y_dev(NY - 1)))

    pad_n = jnp.zeros((LANES - n_rows, 512), BF)

    def wide(ref_val):
        return jnp.concatenate([ref_val, pad_n], axis=0)

    pass_on(0)

    for b in range(nz):
        dyt[b] = dyin[:, :, b * zw:(b + 1) * zw].reshape(rows, zw).T
    order = [4, 3, 5, 2, 6, 1, 7, 0]
    chip = {}

    def down_part(d):
        yt = lax.rem(y + d, NY)
        lo = pl.multiple_of(yt * yw + (1 - core) * cw, cw)
        part = nn(dyt[:, pl.ds(lo, cw), :].reshape(nz * cw, LANES), hg[...])
        gds[d] = part.astype(BF)
        chip[d] = send(gds.at[d], gdr.at[d], c_dev)
        lo = pl.multiple_of(yt * yw + core * cw, cw)
        gdo[d] = nn(dyt[:, pl.ds(lo, cw), :].reshape(nz * cw, LANES), hg[...])

    for d in order[:4]:
        down_part(d)
    pass_on(1)
    for d in order[4:]:
        down_part(d)

    def chip_sum(d):
        chip[d].wait_recv()
        return gdo[d] + gdr[d].astype(F32)

    far = chip_sum(4).astype(BF)
    psend[0] = far
    p_in = [send(psend.at[0, pl.ds(0, half)], p0r, y_dev(1))]
    m_in = [send(psend.at[0, pl.ds(half, half)], m0r, y_dev(NY - 1))]

    lo = pl.multiple_of(y * yw, yw)
    acc = nn(xt[:, pl.ds(lo, yw), :].reshape(nz * yw, LANES), wide(nar[...]))
    gx[...] = acc.reshape(nz, yw, 512)

    def add_factor(d, value):
        x_in[d - 1].wait_recv()
        part = nn(xty[d - 1].reshape(nz * yw, LANES), wide(value))
        gx[...] = gx[...] + part.reshape(nz, yw, 512)

    pass_on(2)
    add_factor(1, gp_in[0])
    add_factor(NY - 1, gm_in[0])

    for copy in back[0]:
        copy.wait_recv()
    for e in range(2):
        zsum[e * SLAB:(e + 1) * SLAB] = (
            ret[2 * e, 0].astype(F32) + ret[2 * e + 1, 0].astype(F32)).astype(BF)
    z_back = send(zsum, zrin, h_dev)

    p_in[0].wait_recv()
    s3 = chip_sum(3)
    psend[1, 0:half] = (s3[0:half] + p0r[...].astype(F32)).astype(BF)
    psend[1, half:] = s3[half:].astype(BF)
    p_in.append(send(psend.at[1], prr.at[0], y_dev(1)))
    m_in[0].wait_recv()
    s5 = chip_sum(5)
    msend[0, 0:half] = s5[0:half].astype(BF)
    msend[0, half:] = (s5[half:] + m0r[...].astype(F32)).astype(BF)
    m_in.append(send(msend.at[0], mrr.at[0], y_dev(NY - 1)))
    add_factor(2, gp_in[1])
    add_factor(NY - 2, gm_in[1])
    add_factor(3, gp_in[2])
    add_factor(NY - 3, gm_in[2])
    p_in[1].wait_recv()
    psend[2] = (chip_sum(2) + prr[0].astype(F32)).astype(BF)
    p_in.append(send(psend.at[2], prr.at[1], y_dev(1)))
    m_in[1].wait_recv()
    msend[1] = (chip_sum(6) + mrr[0].astype(F32)).astype(BF)
    m_in.append(send(msend.at[1], mrr.at[1], y_dev(NY - 1)))
    up[3].wait_recv()
    down[3].wait_recv()
    add_factor(4, g4_in[...])
    lo = pl.multiple_of((1 - core) * cw, cw)
    x_chip = send(gx.at[:, pl.ds(lo, cw), :], gxr, c_dev)
    p_in[2].wait_recv()
    psend[3] = (chip_sum(1) + prr[1].astype(F32)).astype(BF)
    p_in.append(send(psend.at[3], prr.at[2], y_dev(1)))
    m_in[2].wait_recv()
    msend[2] = (chip_sum(7) + mrr[1].astype(F32)).astype(BF)
    m_in.append(send(msend.at[2], mrr.at[2], y_dev(NY - 1)))

    x_chip.wait_recv()
    lo = pl.multiple_of(core * cw, cw)
    sx[...] = gx[:, pl.ds(lo, cw), :] + gxr[...]
    zx_in = []
    for d in range(1, nz):
        zsx[d - 1] = sx[lax.rem(z + d, nz)].astype(BF)
        zx_in.append(send(zsx.at[d - 1], zrx.at[d - 1], z_dev(d)))

    for copy in back[1]:
        copy.wait_recv()
    z_back.wait_recv()
    out = []
    tops, lows = [], []
    for e in range(2):
        total = (ret[2 * e, 1].astype(F32) + ret[2 * e + 1, 1].astype(F32)
                 + zrin[e * SLAB:(e + 1) * SLAB].astype(F32))
        high = total.astype(BF)
        tops.append(high)
        lows.append((total - high.astype(F32)).astype(BF))
        gs2 = total[:, width:]
        gs2 = jnp.concatenate([gs2, gs2], axis=1)
        out.append(jnp.sum(pl_ref[e * SLAB:(e + 1) * SLAB] * gs2, axis=0, keepdims=True))
    gg_ref[0:1] = jnp.where(r0 == 0, out[0], 0.0) + jnp.where(r0 == 1, out[1], 0.0)
    gg_ref[1:2] = jnp.where(r1 == 0, out[0], 0.0) + jnp.where(r1 == 1, out[1], 0.0)
    both = jnp.concatenate(
        tops + lows + [jnp.zeros((LANES - 4 * SLAB, width + LANES), BF)], axis=0)
    stores = []
    for i, c in enumerate(range(0, width, 1024)):
        for c2 in range(c, c + 1024, 512):
            ig[:, c2:c2 + 512] = nn(plt_ref[...], both[:, c2:c2 + 512]).astype(BF)
        store = pltpu.make_async_copy(
            ig.at[:, pl.ds(c, 1024)], ig_hbm.at[:, pl.ds(c, 1024)], loc_sem.at[5 + i])
        store.start()
        stores.append(store)

    p_in[3].wait_recv()
    m_in[3].wait_recv()
    total = chip_sum(0) + prr[2].astype(F32) + mrr[2].astype(F32)
    sd[...] = total.reshape(nz, cw, 256)
    zd_in = []
    for d in range(1, nz):
        zsd[d - 1] = sd[lax.rem(z + d, nz)].astype(BF)
        zd_in.append(send(zsd.at[d - 1], zrd.at[d - 1], z_dev(d)))
    acc = sx[z]
    for d in range(1, nz):
        zx_in[d - 1].wait_recv()
        acc = acc + zrx[d - 1].astype(F32)
    wgr_ref[0] = acc[:, :256]
    wgr_ref[1] = acc[:, 256:]
    acc = sd[z]
    for d in range(1, nz):
        zd_in[d - 1].wait_recv()
        acc = acc + zrd[d - 1].astype(F32)
    wgr_ref[2] = acc
    for store in stores:
        store.wait()
    for copy in started:
        copy.wait_send()


def per_device(grad_out, routes, gate_levels, saved_inputs, w_gate, w_up, w_down):
    group, n_dp = lax.axis_size("expert"), lax.axis_size("dp")
    nx, nz = group // NH, n_dp // (NY * NC)
    n_rows, width = saved_inputs.shape
    cap = n_rows // group
    toks = grad_out.shape[0]
    f = w_gate.shape[1]
    rows = group * SLAB
    ext = width + LANES
    zw = width // nz
    yw = zw // NY
    cw = yw // NC
    own = nz * cw
    V = pltpu.VMEM
    scratch = [
        V((toks, width), BF), V((n_rows, width), BF), V((width, f), BF), V((width, f), BF),
        V((f, width), BF), V((toks, width), BF),
        V((2 * SLAB, toks), F32), V((toks, LANES), BF), V((2 * SLAB, ext), BF),
        V((2 * SLAB, ext), BF), V((group, SLAB, ext), BF), V((rows, width), BF),
        V((nz, zw, LANES), BF), V((NY - 1, nz, yw, LANES), BF),
        V((rows, f), F32), V((rows, f), F32), V((rows, f), F32),
        V((n_rows, 2 * f), BF), V((3, n_rows, 2 * f), BF), V((3, n_rows, 2 * f), BF),
        V((n_rows, 2 * f), BF), V((rows, 2 * f), BF), V((rows, f), BF),
        V((group, SLAB, ext), BF), V((nx, 2, SLAB, ext), BF), V((2 * SLAB, ext), BF),
        V((2 * SLAB, ext), BF), V((nz, zw, LANES), BF),
        V((NY, own, f), BF), V((NY, own, f), BF), V((NY, own, f), F32),
        V((4, own, f), BF), V((3, own, f), BF), V((3, own, f), BF), V((3, own, f), BF),
        V((own // 2, f), BF), V((own // 2, f), BF), V((nz, cw, f), F32),
        V((nz, yw, 2 * f), F32), V((nz, cw, 2 * f), F32), V((nz, cw, 2 * f), F32),
        V((nz - 1, cw, f), BF), V((nz - 1, cw, f), BF),
        V((nz - 1, cw, 2 * f), BF), V((nz - 1, cw, 2 * f), BF),
        pltpu.SemaphoreType.DMA((8,)), pltpu.SemaphoreType.DMA((80,)),
        pltpu.SemaphoreType.DMA((80,)),
    ]
    vm = pl.BlockSpec(memory_space=pltpu.VMEM)
    anywhere = pl.BlockSpec(memory_space=pl.ANY)
    input_grad, gate_grad, weight_grad = pl.pallas_call(
        functools.partial(kernel, nx, nz, cap),
        out_shape=[
            jax.ShapeDtypeStruct((toks, width), BF),
            jax.ShapeDtypeStruct((2, toks), F32),
            jax.ShapeDtypeStruct((3, cw, f), F32),
        ],
        in_specs=[vm, vm] + [anywhere] * 5,
        out_specs=[anywhere, vm, vm],
        scratch_shapes=scratch,
        compiler_params=pltpu.CompilerParams(
            collective_id=0, has_side_effects=True, vmem_limit_bytes=56 * 1024 * 1024),
    )(routes.T, gate_levels.T, grad_out, saved_inputs, w_gate, w_up, w_down)
    return (input_grad, gate_grad.T, jnp.transpose(weight_grad, (1, 0, 2)))


def solution(mesh):
    in_specs = (
        P(("dp", "expert"), None),
        P(("dp", "expert"), None),
        P(("dp", "expert"), None),
        P(("dp", "expert"), None),
        P(None, "expert"),
        P(None, "expert"),
        P("expert", None),
    )
    out_specs = (P(("dp", "expert"), None), P(("dp", "expert"), None), P("dp", None, "expert"))
    return jax.shard_map(
        per_device, mesh=mesh, in_specs=in_specs, out_specs=out_specs, check_vma=False
    )
```

```python
import functools

import jax
import jax.numpy as jnp
from jax import lax
from jax.experimental import pallas as pl
from jax.experimental.pallas import tpu as pltpu
from jax.sharding import PartitionSpec as P

NY, NC, NH = 8, 2, 2
SLAB = 16
LANES = 128
BF, F32 = jnp.bfloat16, jnp.float32


def nt(a, b):
    return lax.dot_general(a, b, (((1,), (1,)), ((), ())), preferred_element_type=F32)


def nn(a, b):
    return lax.dot_general(a, b, (((1,), (0,)), ((), ())), preferred_element_type=F32)


def kernel(
    nx, nz, cap,
    routes_ref, levels_ref, go_hbm, x_hbm, wg_hbm, wu_hbm, wd_hbm,
    both_ref, plt_ref, gg_ref, wgr_ref,
    go, xv, wg, wu, wd,
    pl_ref, pk, pkx, zin, zinx, dyin, xp, xs, xty, act, hid, dfac,
    nar, gp_in, gm_in, g4_in, dab, hg, ip, ret, zsum, zrin, dyt,
    gds, gdr, gdo, psend, prr, msend, mrr, p0r, m0r, sd, gx, gxr, sx,
    zsd, zrd, zsx, zrx, loc_sem, send_sem, recv_sem,
):
    dp, ex = lax.axis_index("dp"), lax.axis_index("expert")
    core = lax.rem(dp, NC)
    y = lax.rem(lax.div(dp, NC), NY)
    z = lax.div(dp, NC * NY)
    h = lax.rem(ex, NH)
    x = lax.div(ex, NH)
    width = go.shape[1]
    rows = dyin.shape[0] * SLAB
    zw = width // nz
    yw = zw // NY
    cw = yw // NC
    half = nz * cw // 2

    def x_dev(d):
        return (dp, lax.rem(x + d, nx) * NH + h)

    h_dev = (dp, x * NH + (1 - h))

    def y_dev(d):
        return ((z * NY + lax.rem(y + d, NY)) * NC + core, ex)

    c_dev = ((z * NY + y) * NC + (1 - core), ex)

    def z_dev(d):
        return ((lax.rem(z + d, nz) * NY + y) * NC + core, ex)

    started = []

    def send(src, dst, dev):
        i = len(started)
        copy = pltpu.make_async_remote_copy(
            src_ref=src, dst_ref=dst, send_sem=send_sem.at[i], recv_sem=recv_sem.at[i],
            device_id=dev, device_id_type=pl.DeviceIdType.MESH,
        )
        copy.start()
        started.append(copy)
        return copy

    quarter = width // 4
    cols = [(k * quarter, quarter + (LANES if k == 3 else 0)) for k in range(4)]
    go_loads = [
        pltpu.make_async_copy(
            go_hbm.at[:, pl.ds(a, quarter)], go.at[:, pl.ds(a, quarter)], loc_sem.at[4 + k])
        for k, (a, _) in enumerate(cols)
    ]
    loads = [
        pltpu.make_async_copy(src, dst, loc_sem.at[i])
        for i, (src, dst) in enumerate([(x_hbm, xv), (wg_hbm, wg), (wu_hbm, wu), (wd_hbm, wd)])
    ]
    for load in go_loads:
        load.start()
    loads[0].start()
    barrier = pltpu.get_barrier_semaphore()
    partners = (
        [h_dev] + [x_dev(d) for d in range(1, nx)] + [y_dev(d) for d in range(1, NY)]
        + [c_dev] + [z_dev(d) for d in range(1, nz)]
    )
    for dev in partners:
        pl.semaphore_signal(barrier, inc=1, device_id=dev, device_id_type=pl.DeviceIdType.MESH)

    toks = go.shape[0]
    r = routes_ref[...]
    lv = levels_ref[...].astype(F32)
    r0, r1, l0, l1 = r[0:1], r[1:2], lv[0:1], lv[1:2]
    mem = [jnp.where((r0 == e) | (r1 == e), 1.0, 0.0) for e in range(2)]
    lev = [jnp.where(r0 == e, l0, 0.0) + jnp.where(r1 == e, l1, 0.0) for e in range(2)]
    row8 = lax.broadcasted_iota(jnp.int32, (8, toks), 0)
    m8 = jnp.where(row8 == 0, mem[0], jnp.where(row8 == 1, mem[1], 0.0)).astype(BF)
    tri = jnp.where(
        lax.broadcasted_iota(jnp.int32, (toks, toks), 0)
        <= lax.broadcasted_iota(jnp.int32, (toks, toks), 1), 1.0, 0.0,
    ).astype(BF)
    slots = nn(m8, tri) - 1.0
    row = lax.broadcasted_iota(jnp.int32, (2 * cap, toks), 0)
    first = row < cap
    want = jnp.where(first, row, row - cap).astype(F32)
    slot_row = jnp.where(first, slots[0:1], slots[1:2])
    mem_row = jnp.where(first, mem[0], mem[1])
    lev_row = jnp.where(first, lev[0], lev[1])
    placed = jnp.where((mem_row > 0.5) & (slot_row == want), 1.0, 0.0)
    pl_ref[...] = placed
    gate = jnp.sum(placed * lev_row, axis=1, keepdims=True) * (1.0 / 16.0)
    pk[:, width:] = jnp.broadcast_to(gate, (2 * cap, LANES)).astype(BF)
    placed_b = placed.astype(BF)

    ei = lax.broadcasted_iota(jnp.int32, (2 * SLAB, 2 * cap), 0)
    ek = lax.broadcasted_iota(jnp.int32, (2 * SLAB, 2 * cap), 1)
    ec = jnp.bitwise_and(ei, SLAB - 1)
    expand = jnp.where(
        (ec < cap) & (ek == jnp.right_shift(ei, 4) * cap + ec), 1.0, 0.0).astype(BF)
    ci = lax.broadcasted_iota(jnp.int32, (2 * cap, nx * SLAB), 0)
    ck = lax.broadcasted_iota(jnp.int32, (2 * cap, nx * SLAB), 1)
    ce = jnp.where(ck < nx * SLAB // 2, 0, 1)
    compact = jnp.where(
        ci == ce * cap + jnp.bitwise_and(ck, SLAB - 1), 1.0, 0.0)
    compact = jnp.where(jnp.bitwise_and(ck, SLAB - 1) < cap, compact, 0.0).astype(BF)

    mine, other = x * NH + h, x * NH + (1 - h)
    z_in = []
    for k, (a, w) in enumerate(cols):
        go_loads[k].wait()
        pk[:, a:a + quarter] = nn(placed_b, go[:, a:a + quarter]).astype(BF)
        if k == 0:
            pl.semaphore_wait(barrier, len(partners))
        z_in.append(send(pk.at[:, pl.ds(a, w)], zin.at[:, pl.ds(a, w)], h_dev))
    for load in loads[1:]:
        load.start()

    loads[0].wait()
    n_rows = xv.shape[0]
    for t in range(NY):
        for b in range(0, nz, 2):
            lo = b * zw + t * yw
            xs[t, :, b * yw:(b + 2) * yw] = jnp.concatenate(
                [xv[:, lo:lo + yw], xv[:, lo + zw:lo + zw + yw]], axis=1)
    x_in = []
    for d in range(1, NY):
        x_in.append(send(xs.at[lax.rem(y + d, NY)], xty.at[d - 1], y_dev(d)))

    def spread(src, slab, a, w):
        got = []
        for d in range(1, nx):
            e = lax.div(lax.rem(x + d, nx), nx // 2)
            lo = pl.multiple_of(e * SLAB, SLAB)
            got.append(send(src.at[pl.ds(lo, SLAB), pl.ds(a, w)],
                            dyin.at[slab, :, pl.ds(a, w)], x_dev(d)))
        return got

    own = pl.multiple_of(lax.div(x, nx // 2) * SLAB, SLAB)
    for a, w in cols:
        pkx[:, a:a + w] = nn(expand, pk[:, a:a + w]).astype(BF)
    dy_own = spread(pkx, mine, 0, width + LANES)
    dyin[mine] = pkx[pl.ds(own, SLAB), :]

    gi = lax.broadcasted_iota(jnp.int32, (rows, n_rows), 0)
    gk = lax.broadcasted_iota(jnp.int32, (rows, n_rows), 1)
    gc = jnp.bitwise_and(gi, SLAB - 1)
    gs = jnp.right_shift(gi, 4)
    widen = jnp.where((gc < cap) & (gk == gs * cap + gc), 1.0, 0.0).astype(BF)
    ni = lax.broadcasted_iota(jnp.int32, (n_rows, rows), 0)
    nk = lax.broadcasted_iota(jnp.int32, (n_rows, rows), 1)
    nc_ = jnp.bitwise_and(nk, SLAB - 1)
    ns = jnp.right_shift(nk, 4)
    narrow = jnp.where((nc_ < cap) & (ni == ns * cap + nc_), 1.0, 0.0).astype(BF)
    for c in range(0, width, 512):
        xp[:, c:c + 512] = nn(widen, xv[:, c:c + 512]).astype(BF)
    loads[1].wait()
    a_pre = nn(xp[...], wg[...])
    loads[2].wait()
    b_pre = nn(xp[...], wu[...])
    sigma = jax.nn.sigmoid(a_pre)
    activ = a_pre * sigma
    act[...] = activ
    hid[...] = activ * b_pre
    dfac[...] = b_pre * sigma * (1.0 + a_pre * (1.0 - sigma))
    pl_two = jnp.concatenate(
        [pl_ref[...], pl_ref[...], jnp.zeros((LANES - 4 * cap, toks), F32)], axis=0)
    plt_ref[...] = pl_two.T[:, :4 * cap].astype(BF)

    loads[3].wait()
    dy_other = []
    for k, (a, w) in enumerate(cols):
        z_in[k].wait_recv()
        zinx[:, a:a + w] = nn(expand, zin[:, a:a + w]).astype(BF)
        dy_other.append(spread(zinx, other, a, w))
    dyin[other] = zinx[pl.ds(own, SLAB), :]
    for copy in dy_own:
        copy.wait_recv()
    proj = jnp.zeros((rows, wd.shape[0]), F32)
    for k, (a, w) in enumerate(cols):
        for copy in dy_other[k]:
            copy.wait_recv()
        proj += nt(dyin[:, :, a:a + quarter].reshape(rows, quarter), wd[:, a:a + quarter])
    g_half = dyin[:, :, width:].reshape(rows, LANES).astype(F32)
    g = jnp.concatenate([g_half, g_half], axis=1)
    d_hid = g * proj
    dab[:, 256:] = (d_hid * act[...]).astype(BF)
    dab[:, :256] = (d_hid * dfac[...]).astype(BF)
    hg[...] = (g * hid[...]).astype(BF)
    gate_part = jnp.sum(hid[...] * proj, axis=1, keepdims=True).astype(BF)

    f = hg.shape[1]
    both_parts = nn(narrow, dab[...]).astype(BF)
    hr = n_rows // 2
    up, down = [], []
    for i in range(2):
        nar[i] = both_parts[:, i * f:(i + 1) * f]
        up.append([send(nar.at[i], gp_in.at[0, i], y_dev(1))])
        down.append([send(nar.at[i], gm_in.at[0, i], y_dev(NY - 1))])

    ip[:, :, width:] = jnp.broadcast_to(gate_part, (rows, LANES)).reshape(dyin.shape[0], SLAB, LANES)
    halves = [(0, width // 2), (width // 2, width // 2 + LANES)]
    back = [[], [], []]
    for k, (a, w) in enumerate(halves):
        for c in range(a, a + width // 2, 512):
            part = nt(dab[:, :256], wg[c:c + 512, :]) + nt(dab[:, 256:], wu[c:c + 512, :])
            ip[:, :, c:c + 512] = part.astype(BF).reshape(dyin.shape[0], SLAB, 512)
        for d in range(1, nx):
            back[k].append(send(ip.at[lax.rem(x + d, nx) * NH + 1 - h, :, pl.ds(a, w)],
                                ret.at[0, x, :, pl.ds(a, w)], x_dev(d)))
    for d in range(1, nx):
        back[2].append(send(ip.at[lax.rem(x + d, nx) * NH + h], ret.at[1, x], x_dev(d)))
    ret[0, x] = ip[x * NH + 1 - h]
    ret[1, x] = ip[x * NH + h]

    def pass_on(k):
        for i in range(2):
            up[i][k].wait_recv()
            if k < 2:
                up[i].append(send(gp_in.at[k, i], gp_in.at[k + 1, i], y_dev(1)))
            else:
                up[i].append(send(gp_in.at[k, i, pl.ds(0, hr)], g4_in.at[i, pl.ds(0, hr)], y_dev(1)))
            down[i][k].wait_recv()
            if k < 2:
                down[i].append(send(gm_in.at[k, i], gm_in.at[k + 1, i], y_dev(NY - 1)))
            else:
                down[i].append(send(
                    gm_in.at[k, i, pl.ds(hr, hr)], g4_in.at[i, pl.ds(hr, hr)], y_dev(NY - 1)))

    pad_n = jnp.zeros((LANES - n_rows, 512), BF)
    pad_x = jnp.zeros((LANES - n_rows, nz * yw), BF)

    def factor(cut, value):
        value = jnp.concatenate([value[0], value[1]], axis=1)
        return nn(jnp.concatenate([cut, pad_x], axis=0).T, jnp.concatenate([value, pad_n], axis=0))

    for b in range(nz):
        dyt[b] = dyin[:, :, b * zw:(b + 1) * zw].reshape(rows, zw).T
    chip = {}

    def down_part(d):
        yt = lax.rem(y + d, NY)
        lo = pl.multiple_of(yt * yw + (1 - core) * cw, cw)
        part = nn(dyt[:, pl.ds(lo, cw), :].reshape(nz * cw, LANES), hg[...])
        gds[d] = part.astype(BF)
        chip[d] = send(gds.at[d], gdr.at[d], c_dev)
        lo = pl.multiple_of(yt * yw + core * cw, cw)
        gdo[d] = nn(dyt[:, pl.ds(lo, cw), :].reshape(nz * cw, LANES), hg[...])

    def chip_sum(d):
        chip[d].wait_recv()
        return gdo[d] + gdr[d].astype(F32)

    for d in (4, 3, 5, 2):
        down_part(d)
    pass_on(0)
    psend[0] = chip_sum(4).astype(BF)
    p_in = [send(psend.at[0, pl.ds(0, half)], p0r, y_dev(1))]
    m_in = [send(psend.at[0, pl.ds(half, half)], m0r, y_dev(NY - 1))]
    for d in (6, 1, 7, 0):
        down_part(d)
    gx[...] = factor(xs[y], nar[...]).reshape(nz, yw, 2 * f)

    def add_factor(d, value):
        x_in[d - 1].wait_recv()
        gx[...] = gx[...] + factor(xty[d - 1], value).reshape(nz, yw, 2 * f)

    z_back = []

    def cross(k):
        a, w = halves[k]
        for copy in back[k]:
            copy.wait_recv()
        zsum[:, a:a + w] = nn(compact, ret[0, :, :, a:a + w].reshape(nx * SLAB, w)).astype(BF)
        z_back.append(send(zsum.at[:, pl.ds(a, w)], zrin.at[:, pl.ds(a, w)], h_dev))

    cross(0)
    pass_on(1)
    cross(1)
    p_in[0].wait_recv()
    s3 = chip_sum(3)
    psend[1, 0:half] = (s3[0:half] + p0r[...].astype(F32)).astype(BF)
    psend[1, half:] = s3[half:].astype(BF)
    p_in.append(send(psend.at[1], prr.at[0], y_dev(1)))
    m_in[0].wait_recv()
    s5 = chip_sum(5)
    msend[0, 0:half] = s5[0:half].astype(BF)
    msend[0, half:] = (s5[half:] + m0r[...].astype(F32)).astype(BF)
    m_in.append(send(msend.at[0], mrr.at[0], y_dev(NY - 1)))
    add_factor(1, gp_in[0])
    add_factor(NY - 1, gm_in[0])
    pass_on(2)
    add_factor(2, gp_in[1])
    add_factor(NY - 2, gm_in[1])
    p_in[1].wait_recv()
    psend[2] = (chip_sum(2) + prr[0].astype(F32)).astype(BF)
    p_in.append(send(psend.at[2], prr.at[1], y_dev(1)))
    m_in[1].wait_recv()
    msend[1] = (chip_sum(6) + mrr[0].astype(F32)).astype(BF)
    m_in.append(send(msend.at[1], mrr.at[1], y_dev(NY - 1)))
    add_factor(3, gp_in[2])
    add_factor(NY - 3, gm_in[2])
    for i in range(2):
        up[i][3].wait_recv()
        down[i][3].wait_recv()
    add_factor(4, g4_in[...])
    lo = pl.multiple_of((1 - core) * cw, cw)
    x_chip = send(gx.at[:, pl.ds(lo, cw), :], gxr, c_dev)
    x_chip.wait_recv()
    lo = pl.multiple_of(core * cw, cw)
    sx[...] = gx[:, pl.ds(lo, cw), :] + gxr[...]
    zx_in = []
    for d in range(1, nz):
        zsx[d - 1] = sx[lax.rem(z + d, nz)].astype(BF)
        zx_in.append(send(zsx.at[d - 1], zrx.at[d - 1], z_dev(d)))

    p_in[2].wait_recv()
    psend[3] = (chip_sum(1) + prr[1].astype(F32)).astype(BF)
    p_in.append(send(psend.at[3], prr.at[2], y_dev(1)))
    m_in[2].wait_recv()
    msend[2] = (chip_sum(7) + mrr[1].astype(F32)).astype(BF)
    m_in.append(send(msend.at[2], mrr.at[2], y_dev(NY - 1)))
    p_in[3].wait_recv()
    m_in[3].wait_recv()
    total = chip_sum(0) + prr[2].astype(F32) + mrr[2].astype(F32)
    sd[...] = total.reshape(nz, cw, 256)
    zd_in = []
    for d in range(1, nz):
        zsd[d - 1] = sd[lax.rem(z + d, nz)].astype(BF)
        zd_in.append(send(zsd.at[d - 1], zrd.at[d - 1], z_dev(d)))

    for copy in back[2]:
        copy.wait_recv()
    for k, (a, w) in enumerate(halves):
        z_back[k].wait_recv()
        total = (nn(compact, ret[1, :, :, a:a + w].reshape(nx * SLAB, w))
                 + zrin[:, a:a + w].astype(F32))
        n = width // 2
        high = total[:, :n].astype(BF)
        both_ref[0:2 * cap, a:a + n] = high
        both_ref[2 * cap:, a:a + n] = (total[:, :n] - high.astype(F32)).astype(BF)
    gs2 = total[:, n:]
    prod = pl_ref[...] * jnp.concatenate([gs2, gs2], axis=1)
    top = lax.broadcasted_iota(jnp.int32, (2 * cap, toks), 0) < cap
    out = [jnp.sum(jnp.where(top, prod, 0.0), axis=0, keepdims=True),
           jnp.sum(jnp.where(top, 0.0, prod), axis=0, keepdims=True)]
    gg_ref[0:1] = jnp.where(r0 == 0, out[0], 0.0) + jnp.where(r0 == 1, out[1], 0.0)
    gg_ref[1:2] = jnp.where(r1 == 0, out[0], 0.0) + jnp.where(r1 == 1, out[1], 0.0)

    acc = sx[z]
    for d in range(1, nz):
        zx_in[d - 1].wait_recv()
        acc = acc + zrx[d - 1].astype(F32)
    wgr_ref[0] = acc[:, :256]
    wgr_ref[1] = acc[:, 256:]
    acc = sd[z]
    for d in range(1, nz):
        zd_in[d - 1].wait_recv()
        acc = acc + zrd[d - 1].astype(F32)
    wgr_ref[2] = acc
    for copy in started:
        copy.wait_send()


def finish(spots_hbm, both_hbm, gg_hbm, wgr_hbm, ig_hbm, gg_out, wgr_out,
           spots, both, ig, gg, wgr, sem):
    width, cut = ig.shape[1], 512
    parts = range(0, width, cut)
    first = pltpu.make_async_copy(spots_hbm, spots, sem.at[0])
    first.start()
    gets = [pltpu.make_async_copy(both_hbm.at[:, pl.ds(c, cut)], both.at[:, pl.ds(c, cut)],
                                  sem.at[5 + i]) for i, c in enumerate(parts)]
    for get in gets:
        get.start()
    get_g = pltpu.make_async_copy(gg_hbm, gg, sem.at[1])
    get_w = pltpu.make_async_copy(wgr_hbm, wgr, sem.at[2])
    get_g.start()
    get_w.start()
    first.wait()
    puts = []
    for i, c in enumerate(parts):
        gets[i].wait()
        ig[:, c:c + cut] = nn(spots[...], both[:, c:c + cut]).astype(BF)
        put = pltpu.make_async_copy(
            ig.at[:, pl.ds(c, cut)], ig_hbm.at[:, pl.ds(c, cut)], sem.at[5 + len(parts) + i])
        put.start()
        puts.append(put)
    get_g.wait()
    get_w.wait()
    puts.append(pltpu.make_async_copy(gg, gg_out, sem.at[3]))
    puts.append(pltpu.make_async_copy(wgr, wgr_out, sem.at[4]))
    for put in puts[-2:]:
        put.start()
    for put in puts:
        put.wait()


def per_device(grad_out, routes, gate_levels, saved_inputs, w_gate, w_up, w_down):
    group, n_dp = lax.axis_size("expert"), lax.axis_size("dp")
    nx, nz = group // NH, n_dp // (NY * NC)
    n_rows, width = saved_inputs.shape
    cap = n_rows // group
    toks = grad_out.shape[0]
    f = w_gate.shape[1]
    rows = group * SLAB
    ext = width + LANES
    zw = width // nz
    yw = zw // NY
    cw = yw // NC
    own = nz * cw
    V = pltpu.VMEM
    scratch = [
        V((toks, width), BF), V((n_rows, width), BF), V((width, f), BF), V((width, f), BF),
        V((f, width), BF),
        V((2 * cap, toks), F32), V((2 * cap, ext), BF), V((2 * SLAB, ext), BF),
        V((2 * cap, ext), BF), V((2 * SLAB, ext), BF), V((group, SLAB, ext), BF),
        V((rows, width), BF),
        V((NY, n_rows, nz * yw), BF), V((NY - 1, n_rows, nz * yw), BF),
        V((rows, f), F32), V((rows, f), F32), V((rows, f), F32),
        V((2, n_rows, f), BF), V((3, 2, n_rows, f), BF), V((3, 2, n_rows, f), BF),
        V((2, n_rows, f), BF), V((rows, 2 * f), BF), V((rows, f), BF),
        V((group, SLAB, ext), BF), V((2, nx, SLAB, ext), BF), V((2 * cap, ext), BF),
        V((2 * cap, ext), BF), V((nz, zw, LANES), BF),
        V((NY, own, f), BF), V((NY, own, f), BF), V((NY, own, f), F32),
        V((4, own, f), BF), V((3, own, f), BF), V((3, own, f), BF), V((3, own, f), BF),
        V((own // 2, f), BF), V((own // 2, f), BF), V((nz, cw, f), F32),
        V((nz, yw, 2 * f), F32), V((nz, cw, 2 * f), F32), V((nz, cw, 2 * f), F32),
        V((nz - 1, cw, f), BF), V((nz - 1, cw, f), BF),
        V((nz - 1, cw, 2 * f), BF), V((nz - 1, cw, 2 * f), BF),
        pltpu.SemaphoreType.DMA((8,)), pltpu.SemaphoreType.DMA((100,)),
        pltpu.SemaphoreType.DMA((100,)),
    ]
    vm = pl.BlockSpec(memory_space=pltpu.VMEM)
    anywhere = pl.BlockSpec(memory_space=pl.ANY)
    both, spots, gate_grad, weight_grad = pl.pallas_call(
        functools.partial(kernel, nx, nz, cap),
        out_shape=[
            jax.ShapeDtypeStruct((4 * cap, width), BF),
            jax.ShapeDtypeStruct((toks, 4 * cap), BF),
            jax.ShapeDtypeStruct((2, toks), F32),
            jax.ShapeDtypeStruct((3, cw, f), F32),
        ],
        in_specs=[vm, vm] + [anywhere] * 5,
        out_specs=[vm, vm, vm, vm],
        scratch_shapes=scratch,
        compiler_params=pltpu.CompilerParams(
            collective_id=0, has_side_effects=True, vmem_limit_bytes=56 * 1024 * 1024),
    )(routes.T, gate_levels.T, grad_out, saved_inputs, w_gate, w_up, w_down)
    input_grad, gate_grad, weight_grad = pl.pallas_call(
        finish,
        out_shape=[
            jax.ShapeDtypeStruct((toks, width), BF),
            jax.ShapeDtypeStruct((2, toks), F32),
            jax.ShapeDtypeStruct((3, cw, f), F32),
        ],
        in_specs=[anywhere] * 4,
        out_specs=[anywhere] * 3,
        scratch_shapes=[
            V((toks, 4 * cap), BF), V((4 * cap, width), BF), V((toks, width), BF),
            V((2, toks), F32), V((3, cw, f), F32), pltpu.SemaphoreType.DMA((20,)),
        ],
    )(spots, both, gate_grad, weight_grad)
    return (input_grad, gate_grad.T, jnp.transpose(weight_grad, (1, 0, 2)))


def solution(mesh):
    in_specs = (
        P(("dp", "expert"), None),
        P(("dp", "expert"), None),
        P(("dp", "expert"), None),
        P(("dp", "expert"), None),
        P(None, "expert"),
        P(None, "expert"),
        P("expert", None),
    )
    out_specs = (P(("dp", "expert"), None), P(("dp", "expert"), None), P("dp", None, "expert"))
    return jax.shard_map(
        per_device, mesh=mesh, in_specs=in_specs, out_specs=out_specs, check_vma=False
    )
```

```python
import functools

import jax
import jax.numpy as jnp
from jax import lax
from jax.experimental import pallas as pl
from jax.experimental.pallas import tpu as pltpu
from jax.sharding import PartitionSpec as P

NY, NC, NH = 8, 2, 2
SLAB = 16
LANES = 128
BF, F32 = jnp.bfloat16, jnp.float32


def nt(a, b):
    return lax.dot_general(a, b, (((1,), (1,)), ((), ())), preferred_element_type=F32)


def nn(a, b):
    return lax.dot_general(a, b, (((1,), (0,)), ((), ())), preferred_element_type=F32)


def kernel(
    nx, nz, cap,
    routes_ref, levels_ref, go_hbm, x_hbm, wg_hbm, wu_hbm, wd_hbm,
    both_hbm, plt_hbm, gg_hbm, wgr_hbm,
    both, plt, gg, wgr, go, xv, wg, wu, wd,
    pl_ref, pk, pkx, zin, zinx, dyin, xp, xs, xty, act, hid, dfac,
    nar, gp_in, gm_in, g4_in, dab, hg, ip, ret, zsum, zrin, dyt,
    gds, gdr, gdo, psend, prr, msend, mrr, p0r, m0r, sd, gx, gxr, sx,
    zsd, zrd, zsx, zrx, loc_sem, send_sem, recv_sem,
):
    dp, ex = lax.axis_index("dp"), lax.axis_index("expert")
    core = lax.rem(dp, NC)
    y = lax.rem(lax.div(dp, NC), NY)
    z = lax.div(dp, NC * NY)
    h = lax.rem(ex, NH)
    x = lax.div(ex, NH)
    width = go.shape[1]
    rows = dyin.shape[0] * SLAB
    zw = width // nz
    yw = zw // NY
    cw = yw // NC
    half = nz * cw // 2

    def x_dev(d):
        return (dp, lax.rem(x + d, nx) * NH + h)

    h_dev = (dp, x * NH + (1 - h))

    def y_dev(d):
        return ((z * NY + lax.rem(y + d, NY)) * NC + core, ex)

    c_dev = ((z * NY + y) * NC + (1 - core), ex)

    def z_dev(d):
        return ((lax.rem(z + d, nz) * NY + y) * NC + core, ex)

    started = []
    puts = []

    def put(src, dst):
        copy = pltpu.make_async_copy(src, dst, loc_sem.at[8 + len(puts)])
        copy.start()
        puts.append(copy)


    def send(src, dst, dev):
        i = len(started)
        copy = pltpu.make_async_remote_copy(
            src_ref=src, dst_ref=dst, send_sem=send_sem.at[i], recv_sem=recv_sem.at[i],
            device_id=dev, device_id_type=pl.DeviceIdType.MESH,
        )
        copy.start()
        started.append(copy)
        return copy

    quarter = width // 4
    cols = [(k * quarter, quarter + (LANES if k == 3 else 0)) for k in range(4)]
    go_loads = [
        pltpu.make_async_copy(
            go_hbm.at[:, pl.ds(a, quarter)], go.at[:, pl.ds(a, quarter)], loc_sem.at[4 + k])
        for k, (a, _) in enumerate(cols)
    ]
    loads = [
        pltpu.make_async_copy(src, dst, loc_sem.at[i])
        for i, (src, dst) in enumerate([(x_hbm, xv), (wg_hbm, wg), (wu_hbm, wu), (wd_hbm, wd)])
    ]
    for load in go_loads:
        load.start()
    loads[0].start()
    barrier = pltpu.get_barrier_semaphore()
    partners = (
        [h_dev] + [x_dev(d) for d in range(1, nx)] + [y_dev(d) for d in range(1, NY)]
        + [c_dev] + [z_dev(d) for d in range(1, nz)]
    )
    for dev in partners:
        pl.semaphore_signal(barrier, inc=1, device_id=dev, device_id_type=pl.DeviceIdType.MESH)

    toks = go.shape[0]
    r = routes_ref[...]
    lv = levels_ref[...].astype(F32)
    r0, r1, l0, l1 = r[0:1], r[1:2], lv[0:1], lv[1:2]
    mem = [jnp.where((r0 == e) | (r1 == e), 1.0, 0.0) for e in range(2)]
    lev = [jnp.where(r0 == e, l0, 0.0) + jnp.where(r1 == e, l1, 0.0) for e in range(2)]
    row8 = lax.broadcasted_iota(jnp.int32, (8, toks), 0)
    m8 = jnp.where(row8 == 0, mem[0], jnp.where(row8 == 1, mem[1], 0.0)).astype(BF)
    tri = jnp.where(
        lax.broadcasted_iota(jnp.int32, (toks, toks), 0)
        <= lax.broadcasted_iota(jnp.int32, (toks, toks), 1), 1.0, 0.0,
    ).astype(BF)
    slots = nn(m8, tri) - 1.0
    row = lax.broadcasted_iota(jnp.int32, (2 * cap, toks), 0)
    first = row < cap
    want = jnp.where(first, row, row - cap).astype(F32)
    slot_row = jnp.where(first, slots[0:1], slots[1:2])
    mem_row = jnp.where(first, mem[0], mem[1])
    lev_row = jnp.where(first, lev[0], lev[1])
    placed = jnp.where((mem_row > 0.5) & (slot_row == want), 1.0, 0.0)
    pl_ref[...] = placed
    gate = jnp.sum(placed * lev_row, axis=1, keepdims=True) * (1.0 / 16.0)
    pk[:, width:] = jnp.broadcast_to(gate, (2 * cap, LANES)).astype(BF)
    placed_b = placed.astype(BF)

    ei = lax.broadcasted_iota(jnp.int32, (2 * SLAB, 2 * cap), 0)
    ek = lax.broadcasted_iota(jnp.int32, (2 * SLAB, 2 * cap), 1)
    ec = jnp.bitwise_and(ei, SLAB - 1)
    expand = jnp.where(
        (ec < cap) & (ek == jnp.right_shift(ei, 4) * cap + ec), 1.0, 0.0).astype(BF)
    ci = lax.broadcasted_iota(jnp.int32, (2 * cap, nx * SLAB), 0)
    ck = lax.broadcasted_iota(jnp.int32, (2 * cap, nx * SLAB), 1)
    ce = jnp.where(ck < nx * SLAB // 2, 0, 1)
    compact = jnp.where(
        ci == ce * cap + jnp.bitwise_and(ck, SLAB - 1), 1.0, 0.0)
    compact = jnp.where(jnp.bitwise_and(ck, SLAB - 1) < cap, compact, 0.0).astype(BF)

    mine, other = x * NH + h, x * NH + (1 - h)
    z_in = []
    for k, (a, w) in enumerate(cols):
        go_loads[k].wait()
        pk[:, a:a + quarter] = nn(placed_b, go[:, a:a + quarter]).astype(BF)
        if k == 0:
            pl.semaphore_wait(barrier, len(partners))
        z_in.append(send(pk.at[:, pl.ds(a, w)], zin.at[:, pl.ds(a, w)], h_dev))
    for load in loads[1:]:
        load.start()

    loads[0].wait()
    n_rows = xv.shape[0]
    for t in range(NY):
        for b in range(0, nz, 2):
            lo = b * zw + t * yw
            xs[t, :, b * yw:(b + 2) * yw] = jnp.concatenate(
                [xv[:, lo:lo + yw], xv[:, lo + zw:lo + zw + yw]], axis=1)
    x_in = []
    for d in range(1, NY):
        x_in.append(send(xs.at[lax.rem(y + d, NY)], xty.at[d - 1], y_dev(d)))

    def spread(src, slab, a, w):
        got = []
        for d in range(1, nx):
            e = lax.div(lax.rem(x + d, nx), nx // 2)
            lo = pl.multiple_of(e * SLAB, SLAB)
            got.append(send(src.at[pl.ds(lo, SLAB), pl.ds(a, w)],
                            dyin.at[slab, :, pl.ds(a, w)], x_dev(d)))
        return got

    own = pl.multiple_of(lax.div(x, nx // 2) * SLAB, SLAB)
    for a, w in cols:
        pkx[:, a:a + w] = nn(expand, pk[:, a:a + w]).astype(BF)
    dy_own = spread(pkx, mine, 0, width + LANES)
    dyin[mine] = pkx[pl.ds(own, SLAB), :]

    gi = lax.broadcasted_iota(jnp.int32, (rows, n_rows), 0)
    gk = lax.broadcasted_iota(jnp.int32, (rows, n_rows), 1)
    gc = jnp.bitwise_and(gi, SLAB - 1)
    gs = jnp.right_shift(gi, 4)
    widen = jnp.where((gc < cap) & (gk == gs * cap + gc), 1.0, 0.0).astype(BF)
    ni = lax.broadcasted_iota(jnp.int32, (n_rows, rows), 0)
    nk = lax.broadcasted_iota(jnp.int32, (n_rows, rows), 1)
    nc_ = jnp.bitwise_and(nk, SLAB - 1)
    ns = jnp.right_shift(nk, 4)
    narrow = jnp.where((nc_ < cap) & (ni == ns * cap + nc_), 1.0, 0.0).astype(BF)
    for c in range(0, width, 512):
        xp[:, c:c + 512] = nn(widen, xv[:, c:c + 512]).astype(BF)
    loads[1].wait()
    a_pre = nn(xp[...], wg[...])
    loads[2].wait()
    b_pre = nn(xp[...], wu[...])
    sigma = jax.nn.sigmoid(a_pre)
    activ = a_pre * sigma
    act[...] = activ
    hid[...] = activ * b_pre
    dfac[...] = b_pre * sigma * (1.0 + a_pre * (1.0 - sigma))
    pl_two = jnp.concatenate(
        [pl_ref[...], pl_ref[...], jnp.zeros((LANES - 4 * cap, toks), F32)], axis=0)
    plt[...] = pl_two.T[:, :4 * cap].astype(BF)
    put(plt, plt_hbm)

    loads[3].wait()
    dy_other = []
    for k, (a, w) in enumerate(cols):
        z_in[k].wait_recv()
        zinx[:, a:a + w] = nn(expand, zin[:, a:a + w]).astype(BF)
        dy_other.append(spread(zinx, other, a, w))
    dyin[other] = zinx[pl.ds(own, SLAB), :]
    for copy in dy_own:
        copy.wait_recv()
    proj = jnp.zeros((rows, wd.shape[0]), F32)
    for k, (a, w) in enumerate(cols):
        for copy in dy_other[k]:
            copy.wait_recv()
        proj += nt(dyin[:, :, a:a + quarter].reshape(rows, quarter), wd[:, a:a + quarter])
    g_half = dyin[:, :, width:].reshape(rows, LANES).astype(F32)
    g = jnp.concatenate([g_half, g_half], axis=1)
    d_hid = g * proj
    dab[:, 256:] = (d_hid * act[...]).astype(BF)
    dab[:, :256] = (d_hid * dfac[...]).astype(BF)
    hg[...] = (g * hid[...]).astype(BF)
    gate_part = jnp.sum(hid[...] * proj, axis=1, keepdims=True).astype(BF)

    f = hg.shape[1]
    both_parts = nn(narrow, dab[...]).astype(BF)
    hr = n_rows // 2
    up, down = [], []
    for i in range(2):
        nar[i] = both_parts[:, i * f:(i + 1) * f]
        up.append([send(nar.at[i], gp_in.at[0, i], y_dev(1))])
        down.append([send(nar.at[i], gm_in.at[0, i], y_dev(NY - 1))])

    ip[:, :, width:] = jnp.broadcast_to(gate_part, (rows, LANES)).reshape(dyin.shape[0], SLAB, LANES)
    back = [[] for _ in range(5)]
    for k, (a, w) in enumerate(cols):
        part = nt(dab[:, :f], wg[a:a + quarter, :]) + nt(dab[:, f:], wu[a:a + quarter, :])
        ip[:, :, a:a + quarter] = part.astype(BF).reshape(dyin.shape[0], SLAB, quarter)
        for d in range(1, nx):
            back[k].append(send(ip.at[lax.rem(x + d, nx) * NH + 1 - h, :, pl.ds(a, w)],
                                ret.at[0, x, :, pl.ds(a, w)], x_dev(d)))
    for d in range(1, nx):
        back[4].append(send(ip.at[lax.rem(x + d, nx) * NH + h], ret.at[1, x], x_dev(d)))
    ret[0, x] = ip[x * NH + 1 - h]
    ret[1, x] = ip[x * NH + h]

    def pass_on(k):
        for i in range(2):
            up[i][k].wait_recv()
            if k < 2:
                up[i].append(send(gp_in.at[k, i], gp_in.at[k + 1, i], y_dev(1)))
            else:
                up[i].append(send(gp_in.at[k, i, pl.ds(0, hr)], g4_in.at[i, pl.ds(0, hr)], y_dev(1)))
            down[i][k].wait_recv()
            if k < 2:
                down[i].append(send(gm_in.at[k, i], gm_in.at[k + 1, i], y_dev(NY - 1)))
            else:
                down[i].append(send(
                    gm_in.at[k, i, pl.ds(hr, hr)], g4_in.at[i, pl.ds(hr, hr)], y_dev(NY - 1)))

    pad_n = jnp.zeros((LANES - n_rows, 512), BF)
    pad_x = jnp.zeros((LANES - n_rows, nz * yw), BF)

    def factor(cut, value):
        value = jnp.concatenate([value[0], value[1]], axis=1)
        return nn(jnp.concatenate([cut, pad_x], axis=0).T, jnp.concatenate([value, pad_n], axis=0))

    for b in range(nz):
        dyt[b] = dyin[:, :, b * zw:(b + 1) * zw].reshape(rows, zw).T
    chip = {}

    def down_part(d):
        yt = lax.rem(y + d, NY)
        lo = pl.multiple_of(yt * yw + (1 - core) * cw, cw)
        part = nn(dyt[:, pl.ds(lo, cw), :].reshape(nz * cw, LANES), hg[...])
        gds[d] = part.astype(BF)
        chip[d] = send(gds.at[d], gdr.at[d], c_dev)
        lo = pl.multiple_of(yt * yw + core * cw, cw)
        gdo[d] = nn(dyt[:, pl.ds(lo, cw), :].reshape(nz * cw, LANES), hg[...])

    def chip_sum(d):
        chip[d].wait_recv()
        return gdo[d] + gdr[d].astype(F32)

    for d in (4, 3, 5, 2):
        down_part(d)
    pass_on(0)
    psend[0] = chip_sum(4).astype(BF)
    p_in = [send(psend.at[0, pl.ds(0, half)], p0r, y_dev(1))]
    m_in = [send(psend.at[0, pl.ds(half, half)], m0r, y_dev(NY - 1))]
    for d in (6, 1, 7, 0):
        down_part(d)
    gx[...] = factor(xs[y], nar[...]).reshape(nz, yw, 2 * f)

    def add_factor(d, value):
        x_in[d - 1].wait_recv()
        gx[...] = gx[...] + factor(xty[d - 1], value).reshape(nz, yw, 2 * f)

    z_back = []

    def cross(k):
        a, w = cols[k]
        for copy in back[k]:
            copy.wait_recv()
        zsum[:, a:a + w] = nn(compact, ret[0, :, :, a:a + w].reshape(nx * SLAB, w)).astype(BF)
        z_back.append(send(zsum.at[:, pl.ds(a, w)], zrin.at[:, pl.ds(a, w)], h_dev))

    cross(0)
    cross(1)
    pass_on(1)
    cross(2)
    cross(3)
    p_in[0].wait_recv()
    s3 = chip_sum(3)
    psend[1, 0:half] = (s3[0:half] + p0r[...].astype(F32)).astype(BF)
    psend[1, half:] = s3[half:].astype(BF)
    p_in.append(send(psend.at[1], prr.at[0], y_dev(1)))
    m_in[0].wait_recv()
    s5 = chip_sum(5)
    msend[0, 0:half] = s5[0:half].astype(BF)
    msend[0, half:] = (s5[half:] + m0r[...].astype(F32)).astype(BF)
    m_in.append(send(msend.at[0], mrr.at[0], y_dev(NY - 1)))
    add_factor(1, gp_in[0])
    add_factor(NY - 1, gm_in[0])
    pass_on(2)
    add_factor(2, gp_in[1])
    add_factor(NY - 2, gm_in[1])
    p_in[1].wait_recv()
    psend[2] = (chip_sum(2) + prr[0].astype(F32)).astype(BF)
    p_in.append(send(psend.at[2], prr.at[1], y_dev(1)))
    m_in[1].wait_recv()
    msend[1] = (chip_sum(6) + mrr[0].astype(F32)).astype(BF)
    m_in.append(send(msend.at[1], mrr.at[1], y_dev(NY - 1)))
    add_factor(3, gp_in[2])
    add_factor(NY - 3, gm_in[2])
    for i in range(2):
        up[i][3].wait_recv()
        down[i][3].wait_recv()
    add_factor(4, g4_in[...])
    lo = pl.multiple_of((1 - core) * cw, cw)
    x_chip = send(gx.at[:, pl.ds(lo, cw), :], gxr, c_dev)
    x_chip.wait_recv()
    lo = pl.multiple_of(core * cw, cw)
    sx[...] = gx[:, pl.ds(lo, cw), :] + gxr[...]
    zx_in = []
    for d in range(1, nz):
        zsx[d - 1] = sx[lax.rem(z + d, nz)].astype(BF)
        zx_in.append(send(zsx.at[d - 1], zrx.at[d - 1], z_dev(d)))

    p_in[2].wait_recv()
    psend[3] = (chip_sum(1) + prr[1].astype(F32)).astype(BF)
    p_in.append(send(psend.at[3], prr.at[2], y_dev(1)))
    m_in[2].wait_recv()
    msend[2] = (chip_sum(7) + mrr[1].astype(F32)).astype(BF)
    m_in.append(send(msend.at[2], mrr.at[2], y_dev(NY - 1)))
    p_in[3].wait_recv()
    m_in[3].wait_recv()
    total = chip_sum(0) + prr[2].astype(F32) + mrr[2].astype(F32)
    sd[...] = total.reshape(nz, cw, 256)
    zd_in = []
    for d in range(1, nz):
        zsd[d - 1] = sd[lax.rem(z + d, nz)].astype(BF)
        zd_in.append(send(zsd.at[d - 1], zrd.at[d - 1], z_dev(d)))

    for copy in back[4]:
        copy.wait_recv()
    for k, (a, w) in enumerate(cols):
        z_back[k].wait_recv()
        total = (nn(compact, ret[1, :, :, a:a + w].reshape(nx * SLAB, w))
                 + zrin[:, a:a + w].astype(F32))
        n = quarter
        high = total[:, :n].astype(BF)
        both[0:2 * cap, a:a + n] = high
        both[2 * cap:, a:a + n] = (total[:, :n] - high.astype(F32)).astype(BF)
    put(both, both_hbm)
    gs2 = total[:, n:]
    prod = pl_ref[...] * jnp.concatenate([gs2, gs2], axis=1)
    top = lax.broadcasted_iota(jnp.int32, (2 * cap, toks), 0) < cap
    out = [jnp.sum(jnp.where(top, prod, 0.0), axis=0, keepdims=True),
           jnp.sum(jnp.where(top, 0.0, prod), axis=0, keepdims=True)]
    gg[0:1] = jnp.where(r0 == 0, out[0], 0.0) + jnp.where(r0 == 1, out[1], 0.0)
    gg[1:2] = jnp.where(r1 == 0, out[0], 0.0) + jnp.where(r1 == 1, out[1], 0.0)
    put(gg, gg_hbm)

    acc = sx[z]
    for d in range(1, nz):
        zx_in[d - 1].wait_recv()
        acc = acc + zrx[d - 1].astype(F32)
    wgr[0] = acc[:, :256]
    wgr[1] = acc[:, 256:]
    acc = sd[z]
    for d in range(1, nz):
        zd_in[d - 1].wait_recv()
        acc = acc + zrd[d - 1].astype(F32)
    wgr[2] = acc
    put(wgr, wgr_hbm)
    for copy in started:
        copy.wait_send()
    for copy in puts:
        copy.wait()


def finish(spots_hbm, both_hbm, gg_hbm, wgr_hbm, ig_hbm, gg_out, wgr_out,
           spots, both, ig, gg, wgr, sem):
    width, cut = ig.shape[1], 512
    parts = range(0, width, cut)
    first = pltpu.make_async_copy(spots_hbm, spots, sem.at[0])
    first.start()
    gets = [pltpu.make_async_copy(both_hbm.at[:, pl.ds(c, cut)], both.at[:, pl.ds(c, cut)],
                                  sem.at[5 + i]) for i, c in enumerate(parts)]
    for get in gets:
        get.start()
    get_g = pltpu.make_async_copy(gg_hbm, gg, sem.at[1])
    get_w = pltpu.make_async_copy(wgr_hbm, wgr, sem.at[2])
    get_g.start()
    get_w.start()
    first.wait()
    puts = []
    for i, c in enumerate(parts):
        gets[i].wait()
        ig[:, c:c + cut] = nn(spots[...], both[:, c:c + cut]).astype(BF)
        put = pltpu.make_async_copy(
            ig.at[:, pl.ds(c, cut)], ig_hbm.at[:, pl.ds(c, cut)], sem.at[5 + len(parts) + i])
        put.start()
        puts.append(put)
    get_g.wait()
    get_w.wait()
    puts.append(pltpu.make_async_copy(gg, gg_out, sem.at[3]))
    puts.append(pltpu.make_async_copy(wgr, wgr_out, sem.at[4]))
    for put in puts[-2:]:
        put.start()
    for put in puts:
        put.wait()


def per_device(grad_out, routes, gate_levels, saved_inputs, w_gate, w_up, w_down):
    group, n_dp = lax.axis_size("expert"), lax.axis_size("dp")
    nx, nz = group // NH, n_dp // (NY * NC)
    n_rows, width = saved_inputs.shape
    cap = n_rows // group
    toks = grad_out.shape[0]
    f = w_gate.shape[1]
    rows = group * SLAB
    ext = width + LANES
    zw = width // nz
    yw = zw // NY
    cw = yw // NC
    own = nz * cw
    V = pltpu.VMEM
    scratch = [
        V((4 * cap, width), BF), V((toks, 4 * cap), BF), V((2, toks), F32), V((3, cw, f), F32),
        V((toks, width), BF), V((n_rows, width), BF), V((width, f), BF), V((width, f), BF),
        V((f, width), BF),
        V((2 * cap, toks), F32), V((2 * cap, ext), BF), V((2 * SLAB, ext), BF),
        V((2 * cap, ext), BF), V((2 * SLAB, ext), BF), V((group, SLAB, ext), BF),
        V((rows, width), BF),
        V((NY, n_rows, nz * yw), BF), V((NY - 1, n_rows, nz * yw), BF),
        V((rows, f), F32), V((rows, f), F32), V((rows, f), F32),
        V((2, n_rows, f), BF), V((3, 2, n_rows, f), BF), V((3, 2, n_rows, f), BF),
        V((2, n_rows, f), BF), V((rows, 2 * f), BF), V((rows, f), BF),
        V((group, SLAB, ext), BF), V((2, nx, SLAB, ext), BF), V((2 * cap, ext), BF),
        V((2 * cap, ext), BF), V((nz, zw, LANES), BF),
        V((NY, own, f), BF), V((NY, own, f), BF), V((NY, own, f), F32),
        V((4, own, f), BF), V((3, own, f), BF), V((3, own, f), BF), V((3, own, f), BF),
        V((own // 2, f), BF), V((own // 2, f), BF), V((nz, cw, f), F32),
        V((nz, yw, 2 * f), F32), V((nz, cw, 2 * f), F32), V((nz, cw, 2 * f), F32),
        V((nz - 1, cw, f), BF), V((nz - 1, cw, f), BF),
        V((nz - 1, cw, 2 * f), BF), V((nz - 1, cw, 2 * f), BF),
        pltpu.SemaphoreType.DMA((16,)), pltpu.SemaphoreType.DMA((100,)),
        pltpu.SemaphoreType.DMA((100,)),
    ]
    vm = pl.BlockSpec(memory_space=pltpu.VMEM)
    anywhere = pl.BlockSpec(memory_space=pl.ANY)
    both, spots, gate_grad, weight_grad = pl.pallas_call(
        functools.partial(kernel, nx, nz, cap),
        out_shape=[
            jax.ShapeDtypeStruct((4 * cap, width), BF),
            jax.ShapeDtypeStruct((toks, 4 * cap), BF),
            jax.ShapeDtypeStruct((2, toks), F32),
            jax.ShapeDtypeStruct((3, cw, f), F32),
        ],
        in_specs=[vm, vm] + [anywhere] * 5,
        out_specs=[anywhere] * 4,
        scratch_shapes=scratch,
        compiler_params=pltpu.CompilerParams(
            collective_id=0, has_side_effects=True, vmem_limit_bytes=56 * 1024 * 1024),
    )(routes.T, gate_levels.T, grad_out, saved_inputs, w_gate, w_up, w_down)
    input_grad, gate_grad, weight_grad = pl.pallas_call(
        finish,
        out_shape=[
            jax.ShapeDtypeStruct((toks, width), BF),
            jax.ShapeDtypeStruct((2, toks), F32),
            jax.ShapeDtypeStruct((3, cw, f), F32),
        ],
        in_specs=[anywhere] * 4,
        out_specs=[anywhere] * 3,
        scratch_shapes=[
            V((toks, 4 * cap), BF), V((4 * cap, width), BF), V((toks, width), BF),
            V((2, toks), F32), V((3, cw, f), F32), pltpu.SemaphoreType.DMA((20,)),
        ],
    )(spots, both, gate_grad, weight_grad)
    return (input_grad, gate_grad.T, jnp.transpose(weight_grad, (1, 0, 2)))


def solution(mesh):
    in_specs = (
        P(("dp", "expert"), None),
        P(("dp", "expert"), None),
        P(("dp", "expert"), None),
        P(("dp", "expert"), None),
        P(None, "expert"),
        P(None, "expert"),
        P("expert", None),
    )
    out_specs = (P(("dp", "expert"), None), P(("dp", "expert"), None), P("dp", None, "expert"))
    return jax.shard_map(
        per_device, mesh=mesh, in_specs=in_specs, out_specs=out_specs, check_vma=False
    )
```
